512 devices in a mesh: row: 16 (over z, y_hi), col: 32 (over x, y_lo, core).
Axes of the slice: x: 4, y: 8 (y_hi: 2, y_lo: 4; y = y_hi * 4 + y_lo), z: 8, core: 2. Of those that a mesh axis runs over, the one named last changes fastest.
Arguments:
- ainv: float32 [4096, 4096], P('row', 'col'), may hold values from -6 to 6
- lpanel: float32 [4096, 3, 512], P('row', None, 'col'), may hold values from -0.125 to 0.125
- kk_inverse: float32 [3, 512, 512], P(None, 'row'), may hold values from -6 to 6
- row_blocks: int32 [3, 32], replicated, may hold values from 0 to 31, as said below
- list_len: int32 [3], replicated, may hold values from 8 to 24
Outputs:
- ainv_ik: float32 [4096, 3, 512], P(('row', 'col'))
- ainv_kk: float32 [3, 512, 512], P(None, 'row')
- ainv_ki: float32 [3, 512, 4096], P(None, 'row', 'col')
The draws below stay inside these ranges and needn't reach their ends.
Inputs may be any that keep to these rules, and one draw needn't show every extreme that they name: `row_blocks`: entries at positions below list_len[s] are distinct tile numbers; later entries repeat the first entry of the row.
All inputs are finite; a program needn't handle non-finite values.
Results may differ from the reference program's by a relative error of at most 0.00008.
Values sent between devices are 32-bit elements; how exact they have to be, the bound alone decides.
No kernel may reach another device: no remote copies, remote signals or barrier semaphores. Data moves between devices by JAX's collectives and lax.ppermute only.
A program may use at most 64 MiB of HBM per device.

```python
import jax
import jax.numpy as jnp
from jax import lax

W = 512
S = 3
TILE = 128
ANC = 4096
NTILES = 32


def draw_list_len(key, part):
    least = NTILES // 4
    most = 3 * NTILES // 4
    base = jax.random.randint(jax.random.fold_in(key, 7), (S,), least, most + 1).astype(jnp.int32)
    order = jax.random.permutation(jax.random.fold_in(key, 8), S).astype(jnp.int32)
    lengths = jnp.where(order == 0, least, jnp.where(order == 1, most, base))
    return lengths.astype(jnp.int32)


def draw_row_blocks(key, part):
    lengths = draw_list_len(key, part)
    tiles = jnp.arange(NTILES, dtype=jnp.int32)
    listed = []
    for index in range(S):
        subkey = jax.random.fold_in(key, 100 + index)
        noise = jax.random.randint(subkey, (NTILES,), 0, NTILES).astype(jnp.int32)
        offset = jax.random.randint(jax.random.fold_in(subkey, 1), (), 0, NTILES).astype(jnp.int32)
        distance = (tiles - offset) % NTILES
        score = (noise - 3 * distance // 4) * NTILES + tiles
        order = jnp.argsort(-score, stable=True).astype(jnp.int32)
        picked = jnp.where(tiles < lengths[index], order, order[0])
        listed.append(picked)
    return jnp.stack(listed).astype(jnp.int32)


def spiked(values, key, source, target, parts, factor):
    owner, partner = [(jnp.arange(values.shape[position]) // (values.shape[position] // parts)).reshape([-1 if axis == position else 1 for axis in range(values.ndim)]) for position in (source, target)]
    chosen = jax.random.permutation(key, parts)[partner]
    strong = (owner == chosen) | (owner == (partner + parts // 2) % parts)
    return jnp.where(strong, factor * values, values)


def levels(own_key, extent, shards, low, top_value):
    level, own = 1.0, jax.random.fold_in(own_key, 6)
    for axis_at, blocks in shards:
        heights = jnp.exp(jax.random.uniform(jax.random.fold_in(own, axis_at), (blocks,), jnp.float32, low / len(shards), top_value / len(shards)))
        level = level * jnp.repeat(heights, extent[axis_at] // blocks).reshape([-1 if axis == axis_at else 1 for axis in range(len(extent))])
    return level


def centred(rng, shape, scale, limit, shards=(), kind=jnp.bfloat16):
    drawn = jax.random.normal(rng, shape, jnp.float32) * scale
    if len(shards) > 0:
        drawn = levels(rng, shape, shards, -0.22, 0.18) * drawn
    return jnp.clip(drawn, min=-limit, max=limit).astype(kind)


def gaussian_with(stream_key, extent, spread, reach, pieces, heavy, kind=jnp.bfloat16):
    drawn = spread * jax.random.normal(stream_key, extent, jnp.float32)
    if pieces:
        drawn = drawn * levels(stream_key, extent, pieces, -0.22, 0.18)
    return jnp.clip(spiked(drawn, jax.random.fold_in(stream_key, 3), *heavy), -reach, reach).astype(kind)


def setup_inputs(seed: int = 0) -> dict:
    streams_of = jax.random.split(jax.random.key(seed), 6)
    ainv = gaussian_with(streams_of[0], (ANC, ANC), 1.0, 6.0, ((0, 16), (1, 32)), (1, 0, 32, 2.75), jnp.float32)
    lpanel = centred(streams_of[1], (ANC, S, W), (ANC // 2) ** -0.5, 0.125, ((0, 16), (2, 32)), jnp.float32)
    kk_inverse = centred(streams_of[2], (S, W, W), 1.0, 6.0, ((1, 16),), jnp.float32)
    row_blocks = draw_row_blocks(jax.random.fold_in(streams_of[5], 71), 0)
    list_len = draw_list_len(jax.random.fold_in(streams_of[5], 71), 0)
    return {"ainv": ainv, "lpanel": lpanel, "kk_inverse": kk_inverse, "row_blocks": row_blocks, "list_len": list_len}


def tile_masks(row_blocks, list_len):
    tiles = jnp.arange(NTILES, dtype=jnp.int32)
    valid = jnp.arange(row_blocks.shape[1], dtype=jnp.int32)[None, :] < list_len[:, None]
    hit = (row_blocks[:, :, None] == tiles[None, None, :]) & valid[:, :, None]
    return jnp.any(hit, axis=1).astype(jnp.float32).T


def reference(ainv, lpanel, kk_inverse, row_blocks, list_len):
    tile_mask = tile_masks(row_blocks, list_len)
    row_mask = jnp.repeat(tile_mask, TILE, axis=0)
    masked = lpanel * row_mask[:, :, None]
    product = jnp.einsum("ij,jsw->isw", ainv, masked, precision=lax.Precision.HIGHEST)
    ainv_ik = -product * row_mask[:, :, None]
    ainv_kk = kk_inverse - jnp.einsum("isv,isw->svw", lpanel, ainv_ik, precision=lax.Precision.HIGHEST)
    ainv_ki = jnp.transpose(ainv_ik, (1, 2, 0))
    return ainv_ik, ainv_kk, ainv_ki
```

```python
import jax
import jax.numpy as jnp
from jax import lax
from jax.sharding import Mesh, PartitionSpec as P

TILE = 128
ROW = ("z", "yh")
COL = ("x", "yl", "core")
HIGHEST = lax.Precision.HIGHEST


def tile_masks(row_blocks, list_len, ntiles):
    tiles = jnp.arange(ntiles, dtype=jnp.int32)
    valid = jnp.arange(row_blocks.shape[1], dtype=jnp.int32)[None, :] < list_len[:, None]
    hit = (row_blocks[:, :, None] == tiles[None, None, :]) & valid[:, :, None]
    return jnp.any(hit, axis=1).astype(jnp.float32)


def exchange(blocks, axes):
    return lax.all_to_all(blocks, axes, split_axis=0, concat_axis=0, tiled=True)


def copies(shard, axes):
    count = lax.axis_size(axes)
    return exchange(jnp.broadcast_to(shard, (count, *shard.shape)), axes)


def shards(ainv, lpanel, kk_inverse, row_blocks, list_len):
    nx, nyl, nrows = lax.axis_size("x"), lax.axis_size("yl"), lax.axis_size(ROW)
    ncore = 2
    nchips = nx * nyl
    groups = nx * ncore
    rows, sibs, width = lpanel.shape
    cols = ainv.shape[1]
    part = cols // nx
    wide = sibs * width
    row_index = lax.axis_index(ROW)
    core = lax.axis_index("core")

    tile_mask = tile_masks(row_blocks, list_len, rows * nrows // TILE)
    picked = lax.dynamic_slice_in_dim(tile_mask, row_index * (rows // TILE), rows // TILE, 1)
    own_mask = jnp.repeat(picked, TILE, axis=1)
    panel_t = jnp.transpose(lpanel, (1, 2, 0)) * own_mask[:, None, :]
    panel_t = panel_t.reshape(wide, rows)

    pieces = panel_t.reshape(wide, ncore, nx, part).transpose(2, 1, 3, 0)
    mine = exchange(pieces.reshape(groups, part, wide), ("x", "core"))
    mine = mine.transpose(1, 0, 2).reshape(part, groups * wide)
    factor = copies(mine, ROW).reshape(nrows * part, groups * wide)

    ainv_t = ainv.T.reshape(nx, 1, part, rows)
    ainv_t = jnp.broadcast_to(ainv_t, (nx, nyl, part, rows)).reshape(nchips, part, rows)
    ainv_t = exchange(ainv_t, ("x", "yl")).reshape(nchips * part, rows)

    panel_all = copies(panel_t, ("x", "yl")).reshape(nchips, sibs, width, rows)

    product = lax.dot_general(factor, ainv_t, (((0,), (0,)), ((), ())), precision=HIGHEST)
    product = exchange(product.reshape(groups, wide, rows), ("x", "core"))
    inv_t = jnp.sum(product, axis=0).reshape(sibs, width, rows) * -own_mask[:, None, :]

    other = lax.ppermute(inv_t, "core", [(0, 1), (1, 0)])
    both = jnp.where(core == 0, jnp.stack([inv_t, other], 1), jnp.stack([other, inv_t], 1))
    both = both.reshape(sibs, ncore * width, rows)

    term = jnp.einsum("rsvi,swi->rsvw", panel_all, both, precision=HIGHEST)
    diag = jnp.sum(exchange(term, ROW), axis=0)
    diag = copies(diag, COL).reshape(nchips, ncore, sibs, width, ncore * width)
    ainv_kk = kk_inverse - diag.transpose(2, 1, 3, 0, 4).reshape(kk_inverse.shape)

    half = lax.dynamic_slice_in_dim(both, core * cols, cols, 2)
    swap = [
        (r * nchips * ncore + 2 * q + h, q * nchips * ncore + 2 * r + h)
        for r in range(nrows)
        for q in range(nchips)
        for h in range(ncore)
    ]
    ainv_ki = lax.ppermute(half, ROW + COL, swap)

    share = rows // (nchips * ncore)
    split = both.reshape(sibs, ncore * width, nchips, ncore, share)
    split = lax.dynamic_index_in_dim(split, core, 3, keepdims=False)
    split = exchange(split.transpose(2, 3, 0, 1), ("x", "yl"))
    ainv_ik = split.transpose(1, 2, 0, 3).reshape(share, sibs, -1)
    return ainv_ik, ainv_kk, ainv_ki


def solution(mesh):
    devices = mesh.devices.reshape(8, 2, 4, 4, 2)
    fine = Mesh(devices, ROW + COL)
    placed = (P(ROW, COL), P(ROW, None, COL), P(None, ROW, None), P(), P())
    return jax.shard_map(
        shards,
        mesh=fine,
        in_specs=placed,
        out_specs=(P(ROW + COL, None, None), P(None, ROW, None), P(None, ROW, COL)),
        check_vma=False,
    )
```

```python
import jax
import jax.numpy as jnp
from jax import lax
from jax.sharding import Mesh, PartitionSpec as P

TILE = 128
NCORE = 2
ROW = ("zh", "zl", "yh")
COL = ("x", "yl", "core")
HIGHEST = lax.Precision.HIGHEST


def tile_masks(row_blocks, list_len, ntiles):
    tiles = jnp.arange(ntiles, dtype=jnp.int32)
    valid = jnp.arange(row_blocks.shape[1], dtype=jnp.int32)[None, :] < list_len[:, None]
    hit = (row_blocks[:, :, None] == tiles[None, None, :]) & valid[:, :, None]
    return jnp.any(hit, axis=1).astype(jnp.float32)


def exchange(blocks, axes):
    return lax.all_to_all(blocks, axes, split_axis=0, concat_axis=0, tiled=True)


def copies(shard, axes):
    count = lax.axis_size(axes)
    return exchange(jnp.broadcast_to(shard, (count, *shard.shape)), axes)


def with_partner(block, core, dim):
    other = lax.ppermute(block, "core", [(0, 1), (1, 0)])
    first = jnp.where(core == 0, block, other)
    second = jnp.where(core == 0, other, block)
    return jnp.stack([first, second], dim)


def digit_swap():
    zh, zl, yh, x, yl = (lax.axis_size(a) for a in ("zh", "zl", "yh", "x", "yl"))
    pairs = []
    for a in range(zh):
        for b in range(zl * yh):
            for c in range(x):
                for d in range(yl * NCORE):
                    source = ((a * zl * yh + b) * x + c) * yl * NCORE + d
                    target = ((c * zl * yh + b) * x + a) * yl * NCORE + d
                    pairs.append((source, target))
    return pairs


def transposed(nrows):
    return [
        ((r * nrows + q) * NCORE + h, (q * nrows + r) * NCORE + h)
        for r in range(nrows)
        for q in range(nrows)
        for h in range(NCORE)
    ]


def shards(ainv, lpanel, kk_inverse, row_blocks, list_len):
    nx, nyl, nrows = lax.axis_size("x"), lax.axis_size("yl"), lax.axis_size(ROW)
    nchips = nx * nyl
    groups = nx * NCORE
    rows, sibs, width = lpanel.shape
    cols = ainv.shape[1]
    wide = sibs * width
    row_index = lax.axis_index(ROW)
    core = lax.axis_index("core")
    yl = lax.axis_index("yl")

    tile_mask = tile_masks(row_blocks, list_len, rows * nrows // TILE)
    picked = lax.dynamic_slice_in_dim(tile_mask, row_index * (rows // TILE), rows // TILE, 1)
    own_mask = jnp.repeat(picked, TILE, axis=1)
    panel_t = jnp.transpose(lpanel, (1, 2, 0)) * own_mask[:, None, :]
    panel_t = panel_t.reshape(wide, rows)

    panel_all = copies(panel_t, ("x", "yl")).reshape(nchips, sibs, width, rows)

    low, high = panel_t[:, :cols], panel_t[:, cols:]
    keep = jnp.where(core == 0, low, high)
    give = jnp.where(core == 0, high, low)
    got = lax.ppermute(give, "core", [(0, 1), (1, 0)])
    pair = jnp.stack([jnp.where(core == 0, keep, got), jnp.where(core == 0, got, keep)])
    pair = lax.ppermute(pair.reshape(NCORE * wide, cols), ROW + COL, digit_swap())
    pair, panel_all = lax.optimization_barrier((pair, panel_all))
    factor = copies(pair, ROW).reshape(nx, nyl, NCORE * wide, cols)

    product = 0.0
    for step in range(nyl):
        block = ainv
        if step > 0:
            block = lax.ppermute(ainv, "yl", [(i, i ^ step) for i in range(nyl)])
        part = lax.dynamic_index_in_dim(factor, yl ^ step, 1, keepdims=False)
        part = part.reshape(nx * NCORE * wide, cols)
        product += lax.dot_general(part, block, (((1,), (1,)), ((), ())), precision=HIGHEST)

    product = exchange(product.reshape(groups, wide, rows), ("x", "core"))
    inv_t = jnp.sum(product, axis=0).reshape(sibs, width, rows) * -own_mask[:, None, :]
    both = with_partner(inv_t, core, 1).reshape(sibs, NCORE * width, rows)

    half = lax.dynamic_slice_in_dim(both, core * cols, cols, 2)
    ainv_ki = lax.ppermute(half, ROW + COL, transposed(nrows))

    term = jnp.einsum("rsvi,swi->rsvw", panel_all, both, precision=HIGHEST)
    diag = jnp.sum(exchange(term.reshape(nrows, -1), ROW), axis=0)

    diag, ainv_ki = lax.optimization_barrier((diag, ainv_ki))

    ncols = nchips * NCORE
    share = rows // ncols
    split = inv_t.reshape(wide, ncols, share).transpose(1, 0, 2).reshape(ncols, wide * share)
    joined = jnp.concatenate([jnp.broadcast_to(diag, (ncols, diag.size)), split], 1)
    joined = exchange(joined, COL)
    diag = joined[:, : diag.size].reshape(nchips, NCORE, sibs, width, NCORE * width)
    ainv_kk = kk_inverse - diag.transpose(2, 1, 3, 0, 4).reshape(kk_inverse.shape)
    split = joined[:, diag.size // ncols :].reshape(ncols, sibs, width, share)
    ainv_ik = split.transpose(3, 1, 0, 2).reshape(share, sibs, -1)
    return ainv_ik, ainv_kk, ainv_ki


def solution(mesh):
    devices = mesh.devices.reshape(4, 2, 2, 4, 4, 2)
    fine = Mesh(devices, ROW + COL)
    placed = (P(ROW, COL), P(ROW, None, COL), P(None, ROW, None), P(), P())
    return jax.shard_map(
        shards,
        mesh=fine,
        in_specs=placed,
        out_specs=(P(ROW + COL, None, None), P(None, ROW, None), P(None, ROW, COL)),
        check_vma=False,
    )
```

```python
import jax
import jax.numpy as jnp
from jax import lax
from jax.sharding import Mesh, PartitionSpec as P

TILE = 128
NCORE = 2
ROW = ("zh", "zl", "yh")
COL = ("xh", "xl", "ylh", "yll", "core")
HIGHEST = lax.Precision.HIGHEST


def tile_masks(row_blocks, list_len, ntiles):
    tiles = jnp.arange(ntiles, dtype=jnp.int32)
    valid = jnp.arange(row_blocks.shape[1], dtype=jnp.int32)[None, :] < list_len[:, None]
    hit = (row_blocks[:, :, None] == tiles[None, None, :]) & valid[:, :, None]
    return jnp.any(hit, axis=1).astype(jnp.float32)


def exchange(blocks, axes):
    return lax.all_to_all(blocks, axes, split_axis=0, concat_axis=0, tiled=True)


def copies(shard, axes):
    count = lax.axis_size(axes)
    return exchange(jnp.broadcast_to(shard, (count, *shard.shape)), axes)


def doubled(block, axis, dim):
    other = lax.ppermute(block, axis, [(0, 1), (1, 0)])
    side = lax.axis_index(axis)
    first = jnp.where(side == 0, block, other)
    second = jnp.where(side == 0, other, block)
    return jnp.concatenate([first, second], dim)


def digit_swap():
    zh, zl, yh = (lax.axis_size(a) for a in ROW)
    x, rest = lax.axis_size(COL[:2]), lax.axis_size(COL[2:])
    pairs = []
    for a in range(zh):
        for b in range(zl * yh):
            for c in range(x):
                for d in range(rest):
                    source = ((a * zl * yh + b) * x + c) * rest + d
                    target = ((c * zl * yh + b) * x + a) * rest + d
                    pairs.append((source, target))
    return pairs


def transposed(nrows, flip):
    return [
        ((r * nrows + q) * NCORE + h, (q * nrows + r) * NCORE + (h ^ flip))
        for r in range(nrows)
        for q in range(nrows)
        for h in range(NCORE)
    ]


def shards(ainv, lpanel, kk_inverse, row_blocks, list_len):
    nx, nyl = lax.axis_size(COL[:2]), lax.axis_size(COL[2:4])
    nrows, ncols = lax.axis_size(ROW), lax.axis_size(COL)
    rows, sibs, width = lpanel.shape
    cols = ainv.shape[1]
    wide = sibs * width
    row_index = lax.axis_index(ROW)
    core = lax.axis_index("core")

    tile_mask = tile_masks(row_blocks, list_len, rows * nrows // TILE)
    picked = lax.dynamic_slice_in_dim(tile_mask, row_index * (rows // TILE), rows // TILE, 1)
    own_mask = jnp.repeat(picked, TILE, axis=1)
    panel = jnp.transpose(lpanel, (1, 2, 0)) * own_mask[:, None, :]
    panel = panel.reshape(wide, rows)

    swapped = lax.ppermute(panel, ROW + COL, digit_swap())
    factor = copies(swapped, ROW)
    factor = factor.reshape(nx, 2, 2, wide, NCORE, cols)
    factor = factor.transpose(0, 3, 4, 2, 1, 5).reshape(nx * wide, nyl * rows)

    for axis in ("ylh", "yll", "core"):
        ainv = doubled(ainv, axis, 1)

    panel_all = panel[None]
    for axis in ("xh", "ylh", "xl", "yll", "core"):
        panel_all = doubled(panel_all, axis, 0)
    panel_all = panel_all.reshape(2, 2, 2, 2, NCORE, sibs, width, rows)

    product = lax.dot_general(factor, ainv, (((1,), (1,)), ((), ())), precision=HIGHEST)
    product = exchange(product.reshape(nx, wide, rows), COL[:2])
    inv_t = jnp.sum(product, axis=0).reshape(sibs, width, rows) * -own_mask[:, None, :]

    low, high = inv_t[:, :, :cols], inv_t[:, :, cols:]
    same = lax.ppermute(jnp.where(core == 0, low, high), ROW + COL, transposed(nrows, 0))
    flip = lax.ppermute(jnp.where(core == 0, high, low), ROW + COL, transposed(nrows, 1))
    ainv_ki = [jnp.where(core == 0, same, flip), jnp.where(core == 0, flip, same)]
    ainv_ki = jnp.concatenate(ainv_ki, 1)

    term = jnp.einsum("abcdesvi,swi->ecdbsavw", panel_all, inv_t, precision=HIGHEST)
    diag = jnp.sum(exchange(term.reshape(nrows, -1), ROW), axis=0)
    diag, ainv_ki = lax.optimization_barrier((diag, ainv_ki))

    share = rows // ncols
    split = inv_t.reshape(wide, ncols, share).transpose(1, 0, 2).reshape(ncols, wide * share)
    joined = jnp.concatenate([jnp.broadcast_to(diag, (ncols, diag.size)), split], 1)
    joined = exchange(joined, COL)
    diag = joined[:, : diag.size].reshape(ncols, sibs, -1, width)
    ainv_kk = kk_inverse - diag.transpose(1, 2, 0, 3).reshape(kk_inverse.shape)
    split = joined[:, diag.size // ncols :].reshape(ncols, sibs, width, share)
    ainv_ik = split.transpose(3, 1, 0, 2).reshape(share, sibs, -1)
    return ainv_ik, ainv_kk, ainv_ki


def solution(mesh):
    devices = mesh.devices.reshape(4, 2, 2, 2, 2, 2, 2, 2)
    fine = Mesh(devices, ROW + COL)
    placed = (P(ROW, COL), P(ROW, None, COL), P(None, ROW, None), P(), P())

    return jax.shard_map(
        shards,
        mesh=fine,
        in_specs=placed,
        out_specs=(P(ROW + COL, None, None), P(None, ROW, None), P(None, ROW, COL)),
        check_vma=False,
    )
```

```python
import jax
import jax.numpy as jnp
from jax import lax
from jax.sharding import Mesh, PartitionSpec as P

TILE = 128
NCORE = 2
ROW = ("zh", "zl", "yh")
COL = ("xh", "xl", "ylh", "yll", "core")
HIGHEST = lax.Precision.HIGHEST


def tile_masks(row_blocks, list_len, ntiles):
    tiles = jnp.arange(ntiles, dtype=jnp.int32)
    valid = jnp.arange(row_blocks.shape[1], dtype=jnp.int32)[None, :] < list_len[:, None]
    hit = (row_blocks[:, :, None] == tiles[None, None, :]) & valid[:, :, None]
    return jnp.any(hit, axis=1).astype(jnp.float32)


def row_mask(tile_mask, row, rows):
    tiles = rows // TILE
    picked = lax.dynamic_slice_in_dim(tile_mask, row * tiles, tiles, 1)
    return jnp.repeat(picked, TILE, axis=1)[:, None, :]


def exchange(blocks, axes):
    return lax.all_to_all(blocks, axes, split_axis=0, concat_axis=0, tiled=True)


def doubled(block, axis, dim):
    other = lax.ppermute(block, axis, [(0, 1), (1, 0)])
    side = lax.axis_index(axis)
    first = jnp.where(side == 0, block, other)
    second = jnp.where(side == 0, other, block)
    return jnp.concatenate([first, second], dim)


def digit_swap():
    zh, zl, yh = (lax.axis_size(a) for a in ROW)
    x, rest = lax.axis_size(COL[:2]), lax.axis_size(COL[2:])
    pairs = []
    for a in range(zh):
        for b in range(zl * yh):
            for c in range(x):
                for d in range(rest):
                    source = ((a * zl * yh + b) * x + c) * rest + d
                    target = ((c * zl * yh + b) * x + a) * rest + d
                    pairs.append((source, target))
    return pairs


def transposed(nrows):
    return [
        ((r * nrows + q) * NCORE + h, (q * nrows + r) * NCORE + h)
        for r in range(nrows)
        for q in range(nrows)
        for h in range(NCORE)
    ]


def shards(ainv, lpanel, kk_inverse, row_blocks, list_len):
    nx = lax.axis_size(COL[:2])
    nrows, ncols = lax.axis_size(ROW), lax.axis_size(COL)
    nchips = ncols // NCORE
    rows, sibs, width = lpanel.shape
    cols = ainv.shape[1]
    wide = sibs * width
    core = lax.axis_index("core")

    panel = jnp.transpose(lpanel, (1, 2, 0)).reshape(wide, rows)
    swapped = lax.ppermute(panel, ROW + COL, digit_swap())

    tile_mask = tile_masks(row_blocks, list_len, rows * nrows // TILE)
    own_mask = row_mask(tile_mask, lax.axis_index(ROW), rows)
    factor_mask = row_mask(tile_mask, lax.axis_index(COL[:2] + ROW[1:]), rows)

    factor = (swapped.reshape(sibs, width, rows) * factor_mask).reshape(wide, rows)
    factor = jnp.broadcast_to(factor, (nrows, wide, rows))
    factor = exchange(factor, ROW).reshape(nx, 2, 2, wide, rows)

    ainv = ainv[None]
    for axis in ("ylh", "yll", "core"):
        ainv = doubled(ainv, axis, 2 if axis == "core" else 0)

    panel_all = panel[None]
    for axis in ("ylh", "yll", "xh", "xl"):
        panel_all = doubled(panel_all, axis, 0)
    panel_all = panel_all.reshape(2, 2, 2, 2, sibs, width, rows)

    product = 0.0
    for high in range(2):
        for low in range(2):
            part = factor[:, high, low].reshape(nx * wide, rows)
            block = ainv[2 * low + high]
            product += lax.dot_general(part, block, (((1,), (1,)), ((), ())), precision=HIGHEST)
    product = product.reshape(nx, 1, wide, rows)
    product = jnp.broadcast_to(product, (nx, NCORE, wide, rows)).reshape(nx * NCORE, wide, rows)
    product = exchange(product, COL[:2] + COL[4:])
    product = jnp.sum(product.reshape(nx, NCORE, wide, rows), axis=0)
    both = product.reshape(NCORE, sibs, width, rows) * -own_mask

    term = jnp.einsum("cebdsvi,kswi->ecdbsvkw", panel_all, both, precision=HIGHEST)
    term = exchange(term.reshape(nrows, -1), ROW)
    diag = jnp.sum(term, axis=0)

    half = lax.dynamic_slice_in_dim(both, core * cols, cols, 3)
    ainv_ki = lax.ppermute(half, ROW + COL, transposed(nrows))
    diag, ainv_ki = lax.optimization_barrier((diag, ainv_ki))
    ainv_ki = ainv_ki.transpose(1, 0, 2, 3).reshape(sibs, NCORE * width, cols)

    share = rows // ncols
    split = jnp.where(core == 0, both[0], both[1]).reshape(wide, ncols, share)
    split = split.transpose(1, 0, 2).reshape(ncols, wide * share)
    joined = jnp.concatenate([jnp.broadcast_to(diag, (ncols, diag.size)), split], 1)
    joined = exchange(joined, COL)
    diag = joined[:, : diag.size].reshape(nchips, NCORE, sibs, width, NCORE * width)
    ainv_kk = kk_inverse - diag.transpose(2, 1, 3, 0, 4).reshape(kk_inverse.shape)
    split = joined[:, diag.size // ncols :].reshape(ncols, sibs, width, share)
    ainv_ik = split.transpose(3, 1, 0, 2).reshape(share, sibs, -1)
    return ainv_ik, ainv_kk, ainv_ki


def solution(mesh):
    devices = mesh.devices.reshape(4, 2, 2, 2, 2, 2, 2, 2)
    fine = Mesh(devices, ROW + COL)
    placed = (P(ROW, COL), P(ROW, None, COL), P(None, ROW, None), P(), P())

    return jax.shard_map(
        shards,
        mesh=fine,
        in_specs=placed,
        out_specs=(P(ROW + COL, None, None), P(None, ROW, None), P(None, ROW, COL)),
        check_vma=False,
    )
```

```python
import jax
import jax.numpy as jnp
from jax import lax
from jax.sharding import Mesh, PartitionSpec as P

TILE = 128
NCORE = 2
ROW = ("zh", "zl", "yh")
COL = ("xh", "xl", "ylh", "yll", "core")
HIGHEST = lax.Precision.HIGHEST


def tile_masks(row_blocks, list_len, ntiles):
    tiles = jnp.arange(ntiles, dtype=jnp.int32)
    valid = jnp.arange(row_blocks.shape[1], dtype=jnp.int32)[None, :] < list_len[:, None]
    hit = (row_blocks[:, :, None] == tiles[None, None, :]) & valid[:, :, None]
    return jnp.any(hit, axis=1).astype(jnp.float32)


def row_mask(tile_mask, row, rows):
    tiles = rows // TILE
    picked = lax.dynamic_slice_in_dim(tile_mask, row * tiles, tiles, 1)
    return jnp.repeat(picked, TILE, axis=1)[:, None, :]


def exchange(blocks, axes):
    return lax.all_to_all(blocks, axes, split_axis=0, concat_axis=0, tiled=True)


def doubled(block, axis, dim):
    other = lax.ppermute(block, axis, [(0, 1), (1, 0)])
    side = lax.axis_index(axis)
    first = jnp.where(side == 0, block, other)
    second = jnp.where(side == 0, other, block)
    return jnp.concatenate([first, second], dim)


def digit_swap(flip):
    zh, zl, yh = (lax.axis_size(a) for a in ROW)
    x, rest = lax.axis_size(COL[:2]), lax.axis_size(COL[2:])
    pairs = []
    for a in range(zh):
        for b in range(zl * yh):
            for c in range(x):
                for d in range(rest):
                    source = ((a * zl * yh + b) * x + c) * rest + d
                    target = ((c * zl * yh + (b ^ flip)) * x + a) * rest + d
                    pairs.append((source, target))
    return pairs


def transposed(nrows):
    return [
        ((r * nrows + q) * NCORE + h, (q * nrows + r) * NCORE + h)
        for r in range(nrows)
        for q in range(nrows)
        for h in range(NCORE)
    ]


def shards(ainv, lpanel, kk_inverse, row_blocks, list_len):
    nx = lax.axis_size(COL[:2])
    nrows, ncols = lax.axis_size(ROW), lax.axis_size(COL)
    nchips = ncols // NCORE
    rows, sibs, width = lpanel.shape
    cols = ainv.shape[1]
    wide = sibs * width
    core = lax.axis_index("core")

    panel = jnp.transpose(lpanel, (1, 2, 0)).reshape(wide, rows)
    yh = lax.axis_index("yh")
    same = lax.ppermute(panel, ROW + COL, digit_swap(0))
    flip = lax.ppermute(panel, ROW + COL, digit_swap(1))

    tile_mask = tile_masks(row_blocks, list_len, rows * nrows // TILE)
    own_mask = row_mask(tile_mask, lax.axis_index(ROW), rows)
    pair_mask = row_mask(tile_mask, lax.axis_index(COL[:2] + ROW[1:2]), 2 * rows)
    pair = [jnp.where(yh == 0, same, flip), jnp.where(yh == 0, flip, same)]
    pair = jnp.concatenate(pair, 1).reshape(sibs, width, 2 * rows) * pair_mask
    pair = pair.reshape(wide, 2 * rows)
    pair = jnp.broadcast_to(pair, (nrows // 2, wide, 2 * rows))
    factor = exchange(pair, ROW[:2]).reshape(nx, 2, wide, 2 * rows)

    ainv = ainv[None]
    for axis in ("ylh", "yll", "core"):
        ainv = doubled(ainv, axis, 2 if axis == "core" else 0)

    panel_all = panel[None]
    for axis in ("ylh", "yll", "xh"):
        panel_all = doubled(panel_all, axis, 0)
    panel_far = lax.ppermute(panel_all, "xl", [(0, 1), (1, 0)])

    product = 0.0
    for high in range(2):
        for low in range(2):
            part = factor[:, high, :, low * rows : (low + 1) * rows].reshape(nx * wide, rows)
            block = ainv[2 * low + high]
            product += lax.dot_general(part, block, (((1,), (1,)), ((), ())), precision=HIGHEST)
    product = product.reshape(nx, 1, wide, rows)
    product = jnp.broadcast_to(product, (nx, NCORE, wide, rows)).reshape(nx * NCORE, wide, rows)
    product = exchange(product, COL[:2] + COL[4:])
    product = jnp.sum(product.reshape(nx, NCORE, wide, rows), axis=0)
    both = product.reshape(NCORE, sibs, width, rows) * -own_mask
    pair = both.transpose(1, 0, 2, 3).reshape(sibs, NCORE * width, rows)

    terms = []
    for source in (panel_all, panel_far):
        source = source.reshape(2, 2, 2, sibs, width, rows)
        terms.append(jnp.einsum("ebdsvi,swi->edbsvw", source, pair, precision=HIGHEST))
    xl = lax.axis_index("xl")
    first = jnp.where(xl == 0, terms[0], terms[1])
    second = jnp.where(xl == 0, terms[1], terms[0])
    term = jnp.stack([first, second], 1)
    term = exchange(term.reshape(nrows, -1), ROW)
    diag = jnp.sum(term, axis=0)

    share = rows // ncols
    split = jnp.where(core == 0, both[0], both[1]).reshape(wide, ncols, share)
    split = split.transpose(1, 0, 2).reshape(ncols, wide * share)
    joined = jnp.concatenate([jnp.broadcast_to(diag, (ncols, diag.size)), split], 1)
    joined = exchange(joined, COL)
    diag = joined[:, : diag.size].reshape(nchips, NCORE, sibs, width, NCORE * width)
    ainv_kk = kk_inverse - diag.transpose(2, 1, 3, 0, 4).reshape(kk_inverse.shape)
    split = joined[:, diag.size // ncols :].reshape(ncols, sibs, width, share)
    ainv_ik = split.transpose(3, 1, 0, 2).reshape(share, sibs, -1)
    half = lax.dynamic_slice_in_dim(pair, core * cols, cols, 2)
    ainv_ki = lax.ppermute(half, ROW + COL, transposed(nrows))
    return ainv_ik, ainv_kk, ainv_ki


def solution(mesh):
    devices = mesh.devices.reshape(4, 2, 2, 2, 2, 2, 2, 2)
    fine = Mesh(devices, ROW + COL)
    placed = (P(ROW, COL), P(ROW, None, COL), P(None, ROW, None), P(), P())

    return jax.shard_map(
        shards,
        mesh=fine,
        in_specs=placed,
        out_specs=(P(ROW + COL, None, None), P(None, ROW, None), P(None, ROW, COL)),
        check_vma=False,
    )
```

```python
import jax
import jax.numpy as jnp
from jax import lax
from jax.sharding import Mesh, PartitionSpec as P

TILE = 128
NCORE = 2
ROW = ("zh", "zl", "yh")
COL = ("xh", "xl", "ylh", "yll", "core")
HIGHEST = lax.Precision.HIGHEST


def tile_masks(row_blocks, list_len, ntiles):
    tiles = jnp.arange(ntiles, dtype=jnp.int32)
    valid = jnp.arange(row_blocks.shape[1], dtype=jnp.int32)[None, :] < list_len[:, None]
    hit = (row_blocks[:, :, None] == tiles[None, None, :]) & valid[:, :, None]
    return jnp.any(hit, axis=1).astype(jnp.float32)


def row_mask(tile_mask, row, rows):
    tiles = rows // TILE
    picked = lax.dynamic_slice_in_dim(tile_mask, row * tiles, tiles, 1)
    return jnp.repeat(picked, TILE, axis=1)[:, None, :]


def exchange(blocks, axes):
    return lax.all_to_all(blocks, axes, split_axis=0, concat_axis=0, tiled=True)


def doubled(block, axis, dim):
    other = lax.ppermute(block, axis, [(0, 1), (1, 0)])
    side = lax.axis_index(axis)
    first = jnp.where(side == 0, block, other)
    second = jnp.where(side == 0, other, block)
    return jnp.concatenate([first, second], dim)


def digit_swap(flip):
    zh, zl, yh = (lax.axis_size(a) for a in ROW)
    x, rest = lax.axis_size(COL[:2]), lax.axis_size(COL[2:])
    pairs = []
    for a in range(zh):
        for b in range(zl * yh):
            for c in range(x):
                for d in range(rest):
                    source = ((a * zl * yh + b) * x + c) * rest + d
                    target = ((c * zl * yh + (b ^ flip)) * x + a) * rest + d
                    pairs.append((source, target))
    return pairs


def transposed(nrows):
    return [
        ((r * nrows + q) * NCORE + h, (q * nrows + r) * NCORE + h)
        for r in range(nrows)
        for q in range(nrows)
        for h in range(NCORE)
    ]


def shards(ainv, lpanel, kk_inverse, row_blocks, list_len):
    nx = lax.axis_size(COL[:2])
    nrows, ncols = lax.axis_size(ROW), lax.axis_size(COL)
    nchips = ncols // NCORE
    rows, sibs, width = lpanel.shape
    cols = ainv.shape[1]
    wide = sibs * width
    core = lax.axis_index("core")

    panel = jnp.transpose(lpanel, (1, 2, 0)).reshape(wide, rows)
    yh = lax.axis_index("yh")
    same = lax.ppermute(panel, ROW + COL, digit_swap(0))
    flip = lax.ppermute(panel, ROW + COL, digit_swap(1))

    tile_mask = tile_masks(row_blocks, list_len, rows * nrows // TILE)
    own_mask = row_mask(tile_mask, lax.axis_index(ROW), rows)
    pair_mask = row_mask(tile_mask, lax.axis_index(COL[:2] + ROW[1:2]), 2 * rows)
    pair = [jnp.where(yh == 0, same, flip), jnp.where(yh == 0, flip, same)]
    pair = jnp.concatenate(pair, 1).reshape(sibs, width, 2 * rows) * pair_mask
    pair = pair.reshape(wide, 2 * rows)
    pair = jnp.broadcast_to(pair, (nrows // 2, wide, 2 * rows))
    factor = exchange(pair, ROW[:2]).reshape(nx, 2, wide, 2 * rows)

    load = jnp.concatenate([ainv, panel[:, :cols], panel[:, cols:]], 0)[None]
    for axis in ("ylh", "yll"):
        load = doubled(load, axis, 0)
    ainv = doubled(load[:, :rows], "core", 2)
    panel_all = jnp.concatenate([load[:, rows : rows + wide], load[:, rows + wide :]], 2)
    panel_all = doubled(panel_all, "xh", 0)
    panel_far = lax.ppermute(panel_all, "xl", [(0, 1), (1, 0)])

    product = 0.0
    for high in range(2):
        for low in range(2):
            part = factor[:, high, :, low * rows : (low + 1) * rows].reshape(nx * wide, rows)
            block = ainv[2 * low + high]
            product += lax.dot_general(part, block, (((1,), (1,)), ((), ())), precision=HIGHEST)
    product = product.reshape(nx, 1, wide, rows)
    product = jnp.broadcast_to(product, (nx, NCORE, wide, rows)).reshape(nx * NCORE, wide, rows)
    product = exchange(product, COL[:2] + COL[4:])
    product = jnp.sum(product.reshape(nx, NCORE, wide, rows), axis=0)
    both = product.reshape(NCORE, sibs, width, rows) * -own_mask
    pair = both.transpose(1, 0, 2, 3).reshape(sibs, NCORE * width, rows)

    terms = []
    for source in (panel_all, panel_far):
        source = source.reshape(2, 2, 2, sibs, width, rows)
        terms.append(jnp.einsum("ebdsvi,swi->edbsvw", source, pair, precision=HIGHEST))
    xl = lax.axis_index("xl")
    first = jnp.where(xl == 0, terms[0], terms[1])
    second = jnp.where(xl == 0, terms[1], terms[0])
    term = jnp.stack([first, second], 1)
    term = exchange(term.reshape(nrows, -1), ROW)
    own = lax.dynamic_slice_in_dim(kk_inverse, core * width, width, 1)
    own = lax.dynamic_slice_in_dim(own, lax.axis_index(COL[:4]) * NCORE * width, NCORE * width, 2)
    diag = own.reshape(-1) - jnp.sum(term, axis=0)

    half = lax.dynamic_slice_in_dim(pair, core * cols, cols, 2)
    ainv_ki = lax.ppermute(half, ROW + COL, transposed(nrows))

    share = rows // ncols
    split = jnp.where(core == 0, both[0], both[1]).reshape(wide, ncols, share)
    split = split.transpose(1, 0, 2).reshape(ncols, wide * share)
    joined = jnp.concatenate([jnp.broadcast_to(diag, (ncols, diag.size)), split], 1)
    joined = exchange(joined, COL)
    diag = joined[:, : own.size].reshape(nchips, NCORE, sibs, width, NCORE * width)
    ainv_kk = diag.transpose(2, 1, 3, 0, 4).reshape(kk_inverse.shape)
    split = joined[:, own.size :].reshape(ncols, sibs, width, share)
    ainv_ik = split.transpose(3, 1, 0, 2).reshape(share, sibs, -1)
    return ainv_ik, ainv_kk, ainv_ki


def solution(mesh):
    devices = mesh.devices.reshape(4, 2, 2, 2, 2, 2, 2, 2)
    fine = Mesh(devices, ROW + COL)
    placed = (P(ROW, COL), P(ROW, None, COL), P(None, ROW, None), P(), P())

    return jax.shard_map(
        shards,
        mesh=fine,
        in_specs=placed,
        out_specs=(P(ROW + COL, None, None), P(None, ROW, None), P(None, ROW, COL)),
        check_vma=False,
    )
```

```python
import jax
import jax.numpy as jnp
from jax import lax
from jax.sharding import Mesh, PartitionSpec as P

TILE = 128
NCORE = 2
ROW = ("zh", "zl", "yh")
COL = ("xh", "xl", "ylh", "yll", "core")
HIGHEST = lax.Precision.HIGHEST


def tile_masks(row_blocks, list_len, ntiles):
    tiles = jnp.arange(ntiles, dtype=jnp.int32)
    valid = jnp.arange(row_blocks.shape[1], dtype=jnp.int32)[None, :] < list_len[:, None]
    hit = (row_blocks[:, :, None] == tiles[None, None, :]) & valid[:, :, None]
    return jnp.any(hit, axis=1).astype(jnp.float32)


def row_mask(tile_mask, row, rows):
    tiles = rows // TILE
    picked = lax.dynamic_slice_in_dim(tile_mask, row * tiles, tiles, 1)
    return jnp.repeat(picked, TILE, axis=1)[:, None, :]


def exchange(blocks, axes):
    return lax.all_to_all(blocks, axes, split_axis=0, concat_axis=0, tiled=True)


def doubled(block, axis, dim):
    other = lax.ppermute(block, axis, [(0, 1), (1, 0)])
    side = lax.axis_index(axis)
    first = jnp.where(side == 0, block, other)
    second = jnp.where(side == 0, other, block)
    return jnp.concatenate([first, second], dim)


def digit_swap():
    zh, zl, yh = (lax.axis_size(a) for a in ROW)
    x, yl = lax.axis_size(COL[:2]), lax.axis_size(COL[2:4])
    pairs = []
    for a in range(zh):
        for b in range(zl * yh):
            for c in range(x):
                for d in range(yl):
                    for h in range(NCORE):
                        source = (((a * zl * yh + b) * x + c) * yl + d) * NCORE + h
                        target = (((a * yl + d) * x + c) * zl * yh + b) * NCORE + h
                        pairs.append((source, target))
    return pairs


def transposed(nrows):
    return [
        ((r * nrows + q) * NCORE + h, (q * nrows + r) * NCORE + h)
        for r in range(nrows)
        for q in range(nrows)
        for h in range(NCORE)
    ]


def shards(ainv, lpanel, kk_inverse, row_blocks, list_len):
    nyl = lax.axis_size(COL[2:4])
    nrows, ncols = lax.axis_size(ROW), lax.axis_size(COL)
    nchips = ncols // NCORE
    rows, sibs, width = lpanel.shape
    cols = ainv.shape[1]
    wide = sibs * width
    core = lax.axis_index("core")

    panel = jnp.transpose(lpanel, (1, 2, 0)).reshape(wide, rows)
    swapped = lax.ppermute(panel, ROW + COL, digit_swap())

    tile_mask = tile_masks(row_blocks, list_len, rows * nrows // TILE)
    own_mask = row_mask(tile_mask, lax.axis_index(ROW), rows)
    factor_mask = row_mask(tile_mask, lax.axis_index(ROW[:1] + COL[2:4]), rows)
    factor = (swapped.reshape(sibs, width, rows) * factor_mask).reshape(wide, rows)
    factor = jnp.broadcast_to(factor, (nrows, wide, rows))
    factor = exchange(factor, ROW).reshape(2, 2, nyl * wide, rows)

    ainv = ainv[None]
    for axis in ("xh", "xl", "core"):
        ainv = doubled(ainv, axis, 2 if axis == "core" else 0)
    panel_all = panel[None]
    for axis in ("ylh", "yll", "xh"):
        panel_all = doubled(panel_all, axis, 0)
    panel_far = lax.ppermute(panel_all, "xl", [(0, 1), (1, 0)])

    product = 0.0
    for high in range(2):
        for low in range(2):
            block = ainv[2 * low + high]
            product += lax.dot_general(
                factor[high, low], block, (((1,), (1,)), ((), ())), precision=HIGHEST
            )
    product = product.reshape(nyl, 1, wide, rows)
    product = jnp.broadcast_to(product, (nyl, NCORE, wide, rows)).reshape(-1, wide, rows)
    product = exchange(product, COL[2:])
    product = jnp.sum(product.reshape(nyl, NCORE, wide, rows), axis=0)
    both = product.reshape(NCORE, sibs, width, rows) * -own_mask
    pair = both.transpose(1, 0, 2, 3).reshape(sibs, NCORE * width, rows)

    terms = []
    for source in (panel_all, panel_far):
        source = source.reshape(2, 2, 2, sibs, width, rows)
        terms.append(jnp.einsum("ebdsvi,swi->edbsvw", source, pair, precision=HIGHEST))
    xl = lax.axis_index("xl")
    first = jnp.where(xl == 0, terms[0], terms[1])
    second = jnp.where(xl == 0, terms[1], terms[0])
    term = jnp.stack([first, second], 1)
    term = exchange(term.reshape(nrows, -1), ROW)
    own = lax.dynamic_slice_in_dim(kk_inverse, core * width, width, 1)
    own = lax.dynamic_slice_in_dim(own, lax.axis_index(COL[:4]) * NCORE * width, NCORE * width, 2)
    diag = own.reshape(-1) - jnp.sum(term, axis=0)

    half = lax.dynamic_slice_in_dim(pair, core * cols, cols, 2)
    ainv_ki = lax.ppermute(half, ROW + COL, transposed(nrows))

    share = rows // ncols
    split = jnp.where(core == 0, both[0], both[1]).reshape(wide, ncols, share)
    split = split.transpose(1, 0, 2).reshape(ncols, wide * share)
    joined = jnp.concatenate([jnp.broadcast_to(diag, (ncols, diag.size)), split], 1)
    joined = exchange(joined, COL)
    diag = joined[:, : own.size].reshape(nchips, NCORE, sibs, width, NCORE * width)
    ainv_kk = diag.transpose(2, 1, 3, 0, 4).reshape(kk_inverse.shape)
    split = joined[:, own.size :].reshape(ncols, sibs, width, share)
    ainv_ik = split.transpose(3, 1, 0, 2).reshape(share, sibs, -1)
    return ainv_ik, ainv_kk, ainv_ki


def solution(mesh):
    devices = mesh.devices.reshape(4, 2, 2, 2, 2, 2, 2, 2)
    fine = Mesh(devices, ROW + COL)
    placed = (P(ROW, COL), P(ROW, None, COL), P(None, ROW, None), P(), P())

    return jax.shard_map(
        shards,
        mesh=fine,
        in_specs=placed,
        out_specs=(P(ROW + COL, None, None), P(None, ROW, None), P(None, ROW, COL)),
        check_vma=False,
    )
```

```python
import jax
import jax.numpy as jnp
from jax import lax
from jax.sharding import Mesh, PartitionSpec as P

TILE = 128
NCORE = 2
ROW = ("zh", "zl", "yh")
COL = ("xh", "xl", "ylh", "yll", "core")
HIGHEST = lax.Precision.HIGHEST


def tile_masks(row_blocks, list_len, ntiles):
    tiles = jnp.arange(ntiles, dtype=jnp.int32)
    valid = jnp.arange(row_blocks.shape[1], dtype=jnp.int32)[None, :] < list_len[:, None]
    hit = (row_blocks[:, :, None] == tiles[None, None, :]) & valid[:, :, None]
    return jnp.any(hit, axis=1).astype(jnp.float32)


def row_mask(tile_mask, row, rows):
    tiles = rows // TILE
    picked = lax.dynamic_slice_in_dim(tile_mask, row * tiles, tiles, 1)
    return jnp.repeat(picked, TILE, axis=1)[:, None, :]


def exchange(blocks, axes):
    return lax.all_to_all(blocks, axes, split_axis=0, concat_axis=0, tiled=True)


def doubled(block, axis, dim):
    other = lax.ppermute(block, axis, [(0, 1), (1, 0)])
    side = lax.axis_index(axis)
    first = jnp.where(side == 0, block, other)
    second = jnp.where(side == 0, other, block)
    return jnp.concatenate([first, second], dim)


def digit_swap():
    zh, zl, yh = (lax.axis_size(a) for a in ROW)
    x, rest = lax.axis_size(COL[:2]), lax.axis_size(COL[2:])
    pairs = []
    for a in range(zh):
        for b in range(zl * yh):
            for c in range(x):
                for d in range(rest):
                    source = ((a * zl * yh + b) * x + c) * rest + d
                    target = ((c * zl * yh + b) * x + a) * rest + d
                    pairs.append((source, target))
    return pairs


def transposed(nrows):
    return [
        ((r * nrows + q) * NCORE + h, (q * nrows + r) * NCORE + h)
        for r in range(nrows)
        for q in range(nrows)
        for h in range(NCORE)
    ]


def shards(ainv, lpanel, kk_inverse, row_blocks, list_len):
    nx = lax.axis_size(COL[:2])
    nrows, ncols = lax.axis_size(ROW), lax.axis_size(COL)
    nchips = ncols // NCORE
    rows, sibs, width = lpanel.shape
    cols = ainv.shape[1]
    wide = sibs * width
    core = lax.axis_index("core")

    panel = jnp.transpose(lpanel, (1, 2, 0)).reshape(wide, rows)
    swapped = lax.ppermute(panel, ROW + COL, digit_swap())

    tile_mask = tile_masks(row_blocks, list_len, rows * nrows // TILE)
    own_mask = row_mask(tile_mask, lax.axis_index(ROW), rows)
    factor_mask = row_mask(tile_mask, lax.axis_index(COL[:2] + ROW[1:]), rows)
    factor = (swapped.reshape(sibs, width, rows) * factor_mask).reshape(wide, rows)
    factor = jnp.broadcast_to(factor, (nrows, wide, rows))
    factor = exchange(factor, ROW).reshape(nx, 2, 2, wide, rows)

    ainv = ainv[None]
    for axis in ("ylh", "yll", "core"):
        ainv = doubled(ainv, axis, 2 if axis == "core" else 0)
    panel_all = panel[None]
    for axis in ("ylh", "xh", "xl"):
        panel_all = doubled(panel_all, axis, 0)
    panel_far = lax.ppermute(panel_all, "yll", [(0, 1), (1, 0)])

    product = 0.0
    for high in range(2):
        for low in range(2):
            block = ainv[2 * low + high]
            part = factor[:, high, low].reshape(nx * wide, rows)
            product += lax.dot_general(part, block, (((1,), (1,)), ((), ())), precision=HIGHEST)
    product = product.reshape(nx, 1, wide, rows)
    product = jnp.broadcast_to(product, (nx, NCORE, wide, rows)).reshape(-1, wide, rows)
    product = exchange(product, COL[:2] + COL[4:])
    product = jnp.sum(product.reshape(nx, NCORE, wide, rows), axis=0)
    both = product.reshape(NCORE, sibs, width, rows) * -own_mask
    pair = both.transpose(1, 0, 2, 3).reshape(sibs, NCORE * width, rows)

    terms = []
    for source in (panel_all, panel_far):
        source = source.reshape(2, 2, 2, sibs, width, rows)
        terms.append(jnp.einsum("cedsvi,swi->ecdsvw", source, pair, precision=HIGHEST))
    yll = lax.axis_index("yll")
    first = jnp.where(yll == 0, terms[0], terms[1])
    second = jnp.where(yll == 0, terms[1], terms[0])
    term = jnp.stack([first, second], 3)
    term = exchange(term.reshape(nrows, -1), ROW)
    own = lax.dynamic_slice_in_dim(kk_inverse, core * width, width, 1)
    own = lax.dynamic_slice_in_dim(own, lax.axis_index(COL[:4]) * NCORE * width, NCORE * width, 2)
    diag = own.reshape(-1) - jnp.sum(term, axis=0)

    half = lax.dynamic_slice_in_dim(pair, core * cols, cols, 2)
    ainv_ki = lax.ppermute(half, ROW + COL, transposed(nrows))

    share = rows // ncols
    split = jnp.where(core == 0, both[0], both[1]).reshape(wide, ncols, share)
    split = split.transpose(1, 0, 2).reshape(ncols, wide * share)
    joined = jnp.concatenate([jnp.broadcast_to(diag, (ncols, diag.size)), split], 1)
    joined = exchange(joined, COL)
    diag = joined[:, : own.size].reshape(nchips, NCORE, sibs, width, NCORE * width)
    ainv_kk = diag.transpose(2, 1, 3, 0, 4).reshape(kk_inverse.shape)
    split = joined[:, own.size :].reshape(ncols, sibs, width, share)
    ainv_ik = split.transpose(3, 1, 0, 2).reshape(share, sibs, -1)
    return ainv_ik, ainv_kk, ainv_ki


def solution(mesh):
    devices = mesh.devices.reshape(4, 2, 2, 2, 2, 2, 2, 2)
    fine = Mesh(devices, ROW + COL)
    placed = (P(ROW, COL), P(ROW, None, COL), P(None, ROW, None), P(), P())

    return jax.shard_map(
        shards,
        mesh=fine,
        in_specs=placed,
        out_specs=(P(ROW + COL, None, None), P(None, ROW, None), P(None, ROW, COL)),
        check_vma=False,
    )
```

```python
import jax
import jax.numpy as jnp
from jax import lax
from jax.sharding import Mesh, PartitionSpec as P

TILE = 128
NCORE = 2
ROW = ("zh", "zl", "yh")
COL = ("xh", "xl", "ylh", "yll", "core")
HIGHEST = lax.Precision.HIGHEST


def tile_masks(row_blocks, list_len, ntiles):
    tiles = jnp.arange(ntiles, dtype=jnp.int32)
    valid = jnp.arange(row_blocks.shape[1], dtype=jnp.int32)[None, :] < list_len[:, None]
    hit = (row_blocks[:, :, None] == tiles[None, None, :]) & valid[:, :, None]
    return jnp.any(hit, axis=1).astype(jnp.float32)


def row_mask(tile_mask, row, rows):
    tiles = rows // TILE
    picked = lax.dynamic_slice_in_dim(tile_mask, row * tiles, tiles, 1)
    return jnp.repeat(picked, TILE, axis=1)[:, None, :]


def exchange(blocks, axes):
    return lax.all_to_all(blocks, axes, split_axis=0, concat_axis=0, tiled=True)


def doubled(block, axis, dim):
    other = lax.ppermute(block, axis, [(0, 1), (1, 0)])
    side = lax.axis_index(axis)
    first = jnp.where(side == 0, block, other)
    second = jnp.where(side == 0, other, block)
    return jnp.concatenate([first, second], dim)


def digit_swap():
    zh, zl, yh = (lax.axis_size(a) for a in ROW)
    x, yl = lax.axis_size(COL[:2]), lax.axis_size(COL[2:4])
    pairs = []
    for a in range(zh):
        for b in range(zl * yh):
            for c in range(x):
                for d in range(yl):
                    for h in range(NCORE):
                        source = (((a * zl * yh + b) * x + c) * yl + d) * NCORE + h
                        target = (((a * yl + d) * x + c) * zl * yh + b) * NCORE + h
                        pairs.append((source, target))
    return pairs


def transposed(nrows):
    return [
        ((r * nrows + q) * NCORE + h, (q * nrows + r) * NCORE + h)
        for r in range(nrows)
        for q in range(nrows)
        for h in range(NCORE)
    ]


def shards(ainv, lpanel, kk_inverse, row_blocks, list_len):
    nyl = lax.axis_size(COL[2:4])
    nrows, ncols = lax.axis_size(ROW), lax.axis_size(COL)
    nchips = ncols // NCORE
    rows, sibs, width = lpanel.shape
    cols = ainv.shape[1]
    wide = sibs * width
    core = lax.axis_index("core")

    panel = jnp.transpose(lpanel, (1, 2, 0)).reshape(wide, rows)
    swapped = lax.ppermute(panel, ROW + COL, digit_swap())

    tile_mask = tile_masks(row_blocks, list_len, rows * nrows // TILE)
    own_mask = row_mask(tile_mask, lax.axis_index(ROW), rows)
    factor_mask = row_mask(tile_mask, lax.axis_index(ROW[:1] + COL[2:4]), rows)
    factor = (swapped.reshape(sibs, width, rows) * factor_mask).reshape(wide, rows)
    factor = jnp.broadcast_to(factor, (nrows, wide, rows))
    factor = exchange(factor, ROW).reshape(2, 2, nyl * wide, rows)

    ainv = ainv[None]
    for axis in ("xh", "xl", "core"):
        ainv = doubled(ainv, axis, 2 if axis == "core" else 0)
    panel_all = panel[None]
    for axis in ("ylh", "yll", "xh"):
        panel_all = doubled(panel_all, axis, 0)
    panel_far = lax.ppermute(panel_all, "xl", [(0, 1), (1, 0)])

    product = 0.0
    for high in range(2):
        for low in range(2):
            block = ainv[2 * low + high]
            product += lax.dot_general(
                factor[high, low], block, (((1,), (1,)), ((), ())), precision=HIGHEST
            )
    product = exchange(product.reshape(nyl, wide, rows), COL[2:4])
    plain = jnp.sum(product, axis=0)
    other = lax.ppermute(plain, "core", [(0, 1), (1, 0)])
    pair = [jnp.where(core == 0, plain, other), jnp.where(core == 0, other, plain)]
    pair = [block.reshape(sibs, width, rows) for block in pair]
    pair = -jnp.concatenate(pair, 1)
    half = lax.dynamic_slice_in_dim(pair, core * cols, cols, 2)
    pair = pair * own_mask

    terms = []
    for source in (panel_all, panel_far):
        source = source.reshape(2, 2, 2, sibs, width, rows)
        terms.append(jnp.einsum("ebdsvi,swi->edbsvw", source, pair, precision=HIGHEST))
    xl = lax.axis_index("xl")
    first = jnp.where(xl == 0, terms[0], terms[1])
    second = jnp.where(xl == 0, terms[1], terms[0])
    term = jnp.stack([first, second], 1)
    term = exchange(term.reshape(nrows, -1), ROW)
    own = lax.dynamic_slice_in_dim(kk_inverse, core * width, width, 1)
    own = lax.dynamic_slice_in_dim(own, lax.axis_index(COL[:4]) * NCORE * width, NCORE * width, 2)
    diag = own.reshape(-1) - jnp.sum(term, axis=0)

    ainv_ki = lax.ppermute(half, ROW + COL, transposed(nrows))
    tile = lax.dynamic_slice_in_dim(tile_mask, lax.axis_index(COL), 1, 1)
    ainv_ki = ainv_ki * tile[:, :, None]

    share = rows // ncols
    split = -plain.reshape(sibs, width, rows) * own_mask
    split = split.reshape(wide, ncols, share).transpose(1, 0, 2).reshape(ncols, wide * share)
    joined = jnp.concatenate([jnp.broadcast_to(diag, (ncols, diag.size)), split], 1)
    joined = exchange(joined, COL)
    diag = joined[:, : own.size].reshape(nchips, NCORE, sibs, width, NCORE * width)
    ainv_kk = diag.transpose(2, 1, 3, 0, 4).reshape(kk_inverse.shape)
    split = joined[:, own.size :].reshape(ncols, sibs, width, share)
    ainv_ik = split.transpose(3, 1, 0, 2).reshape(share, sibs, -1)
    return ainv_ik, ainv_kk, ainv_ki


def solution(mesh):
    devices = mesh.devices.reshape(4, 2, 2, 2, 2, 2, 2, 2)
    fine = Mesh(devices, ROW + COL)
    placed = (P(ROW, COL), P(ROW, None, COL), P(None, ROW, None), P(), P())

    return jax.shard_map(
        shards,
        mesh=fine,
        in_specs=placed,
        out_specs=(P(ROW + COL, None, None), P(None, ROW, None), P(None, ROW, COL)),
        check_vma=False,
    )
```

```python
import jax
import jax.numpy as jnp
from jax import lax
from jax.sharding import Mesh, PartitionSpec as P

TILE = 128
NCORE = 2
ROW = ("zh", "zl", "yh")
COL = ("xh", "xl", "ylh", "yll", "core")
HIGHEST = lax.Precision.HIGHEST


def tile_masks(row_blocks, list_len, ntiles):
    tiles = jnp.arange(ntiles, dtype=jnp.int32)
    valid = jnp.arange(row_blocks.shape[1], dtype=jnp.int32)[None, :] < list_len[:, None]
    hit = (row_blocks[:, :, None] == tiles[None, None, :]) & valid[:, :, None]
    return jnp.any(hit, axis=1).astype(jnp.float32)


def row_mask(tile_mask, row, rows):
    tiles = rows // TILE
    picked = lax.dynamic_slice_in_dim(tile_mask, row * tiles, tiles, 1)
    return jnp.repeat(picked, TILE, axis=1)[:, None, :]


def exchange(blocks, axes):
    return lax.all_to_all(blocks, axes, split_axis=0, concat_axis=0, tiled=True)


def doubled(block, axis, dim):
    other = lax.ppermute(block, axis, [(0, 1), (1, 0)])
    side = lax.axis_index(axis)
    first = jnp.where(side == 0, block, other)
    second = jnp.where(side == 0, other, block)
    return jnp.concatenate([first, second], dim)


def digit_swap(flip):
    zh, zl, yh = (lax.axis_size(a) for a in ROW)
    x, yl = lax.axis_size(COL[:2]), lax.axis_size(COL[2:4])
    pairs = []
    for a in range(zh):
        for b in range(zl * yh):
            for c in range(x):
                for d in range(yl):
                    for h in range(NCORE):
                        source = (((a * zl * yh + b) * x + c) * yl + d) * NCORE + h
                        target = (((a * yl + (d ^ flip)) * x + c) * zl * yh + b) * NCORE + h
                        pairs.append((source, target))
    return pairs


def transposed(nrows):
    return [
        ((r * nrows + q) * NCORE + h, (q * nrows + r) * NCORE + h)
        for r in range(nrows)
        for q in range(nrows)
        for h in range(NCORE)
    ]


def shards(ainv, lpanel, kk_inverse, row_blocks, list_len):
    nyl = lax.axis_size(COL[2:4])
    nrows, ncols = lax.axis_size(ROW), lax.axis_size(COL)
    nchips = ncols // NCORE
    rows, sibs, width = lpanel.shape
    cols = ainv.shape[1]
    wide = sibs * width
    core = lax.axis_index("core")

    panel = jnp.transpose(lpanel, (1, 2, 0)).reshape(wide, rows)
    yh = lax.axis_index("yh")
    same = lax.ppermute(panel, ROW + COL, digit_swap(0))
    flip = lax.ppermute(panel, ROW + COL, digit_swap(1))

    tile_mask = tile_masks(row_blocks, list_len, rows * nrows // TILE)
    own_mask = row_mask(tile_mask, lax.axis_index(ROW), rows)
    factor_mask = row_mask(tile_mask, lax.axis_index(ROW[:1] + COL[2:4]), rows)
    factor = jnp.stack([jnp.where(yh == 0, same, flip), jnp.where(yh == 0, flip, same)])
    factor = factor.reshape(2, sibs, width, rows) * factor_mask
    factor = jnp.broadcast_to(factor.reshape(2 * wide, rows), (nrows // 2, 2 * wide, rows))
    factor = exchange(factor, ROW[:2]).reshape(2, 2, nyl * wide, rows)

    ainv = ainv[None]
    for axis in ("xh", "xl", "core"):
        ainv = doubled(ainv, axis, 2 if axis == "core" else 0)
    panel_all = panel[None]
    for axis in ("ylh", "yll", "xh"):
        panel_all = doubled(panel_all, axis, 0)
    panel_far = lax.ppermute(panel_all, "xl", [(0, 1), (1, 0)])

    product = 0.0
    for high in range(2):
        for low in range(2):
            block = ainv[2 * low + high]
            product += lax.dot_general(
                factor[high, low], block, (((1,), (1,)), ((), ())), precision=HIGHEST
            )
    product = exchange(product.reshape(nyl, wide, rows), COL[2:4])
    plain = jnp.sum(product, axis=0)
    other = lax.ppermute(plain, "core", [(0, 1), (1, 0)])
    pair = [jnp.where(core == 0, plain, other), jnp.where(core == 0, other, plain)]
    pair = [block.reshape(sibs, width, rows) for block in pair]
    pair = -jnp.concatenate(pair, 1)
    half = lax.dynamic_slice_in_dim(pair, core * cols, cols, 2)
    pair = pair * own_mask

    terms = []
    for source in (panel_all, panel_far):
        source = source.reshape(2, 2, 2, sibs, width, rows)
        terms.append(jnp.einsum("ebdsvi,swi->edbsvw", source, pair, precision=HIGHEST))
    xl = lax.axis_index("xl")
    first = jnp.where(xl == 0, terms[0], terms[1])
    second = jnp.where(xl == 0, terms[1], terms[0])
    term = jnp.stack([first, second], 1)
    term = exchange(term.reshape(nrows, -1), ROW)
    own = lax.dynamic_slice_in_dim(kk_inverse, core * width, width, 1)
    own = lax.dynamic_slice_in_dim(own, lax.axis_index(COL[:4]) * NCORE * width, NCORE * width, 2)
    diag = own.reshape(-1) - jnp.sum(term, axis=0)

    ainv_ki = lax.ppermute(half, ROW + COL, transposed(nrows))
    tile = lax.dynamic_slice_in_dim(tile_mask, lax.axis_index(COL), 1, 1)
    ainv_ki = ainv_ki * tile[:, :, None]

    share = rows // ncols
    split = -plain.reshape(sibs, width, rows) * own_mask
    split = split.reshape(wide, ncols, share).transpose(1, 0, 2).reshape(ncols, wide * share)
    joined = jnp.concatenate([jnp.broadcast_to(diag, (ncols, diag.size)), split], 1)
    joined = exchange(joined, COL)
    diag = joined[:, : own.size].reshape(nchips, NCORE, sibs, width, NCORE * width)
    ainv_kk = diag.transpose(2, 1, 3, 0, 4).reshape(kk_inverse.shape)
    split = joined[:, own.size :].reshape(ncols, sibs, width, share)
    ainv_ik = split.transpose(3, 1, 0, 2).reshape(share, sibs, -1)
    return ainv_ik, ainv_kk, ainv_ki


def solution(mesh):
    devices = mesh.devices.reshape(4, 2, 2, 2, 2, 2, 2, 2)
    fine = Mesh(devices, ROW + COL)
    placed = (P(ROW, COL), P(ROW, None, COL), P(None, ROW, None), P(), P())

    return jax.shard_map(
        shards,
        mesh=fine,
        in_specs=placed,
        out_specs=(P(ROW + COL, None, None), P(None, ROW, None), P(None, ROW, COL)),
        check_vma=False,
    )
```

```python
import jax
import jax.numpy as jnp
from jax import lax
from jax.sharding import Mesh, PartitionSpec as P

TILE = 128
NCORE = 2
ROW = ("zh", "zl", "yh")
COL = ("xh", "xl", "ylh", "yll", "core")
HIGHEST = lax.Precision.HIGHEST


def tile_masks(row_blocks, list_len, ntiles):
    tiles = jnp.arange(ntiles, dtype=jnp.int32)
    valid = jnp.arange(row_blocks.shape[1], dtype=jnp.int32)[None, :] < list_len[:, None]
    hit = (row_blocks[:, :, None] == tiles[None, None, :]) & valid[:, :, None]
    return jnp.any(hit, axis=1).astype(jnp.float32)


def row_mask(tile_mask, row, rows):
    tiles = rows // TILE
    picked = lax.dynamic_slice_in_dim(tile_mask, row * tiles, tiles, 1)
    return jnp.repeat(picked, TILE, axis=1)[:, None, :]


def exchange(blocks, axes):
    return lax.all_to_all(blocks, axes, split_axis=0, concat_axis=0, tiled=True)


def doubled(block, axis, dim):
    other = lax.ppermute(block, axis, [(0, 1), (1, 0)])
    side = lax.axis_index(axis)
    first = jnp.where(side == 0, block, other)
    second = jnp.where(side == 0, other, block)
    return jnp.concatenate([first, second], dim)


def digit_swap(flip):
    zh, zl, yh = (lax.axis_size(a) for a in ROW)
    x, yl = lax.axis_size(COL[:2]), lax.axis_size(COL[2:4])
    pairs = []
    for a in range(zh):
        for b in range(zl * yh):
            for c in range(x):
                for d in range(yl):
                    for h in range(NCORE):
                        source = (((a * zl * yh + b) * x + c) * yl + d) * NCORE + h
                        target = (((a * yl + (d ^ flip)) * x + c) * zl * yh + b) * NCORE + h
                        pairs.append((source, target))
    return pairs


def transposed(nrows):
    return [
        ((r * nrows + q) * NCORE + h, (q * nrows + r) * NCORE + h)
        for r in range(nrows)
        for q in range(nrows)
        for h in range(NCORE)
    ]


def shards(ainv, lpanel, kk_inverse, row_blocks, list_len):
    nyl = lax.axis_size(COL[2:4])
    nrows, ncols = lax.axis_size(ROW), lax.axis_size(COL)
    nchips = ncols // NCORE
    rows, sibs, width = lpanel.shape
    cols = ainv.shape[1]
    wide = sibs * width
    core = lax.axis_index("core")

    panel = jnp.transpose(lpanel, (1, 2, 0)).reshape(wide, rows)
    yh = lax.axis_index("yh")
    same = lax.ppermute(panel, ROW + COL, digit_swap(0))
    flip = lax.ppermute(panel, ROW + COL, digit_swap(1))

    tile_mask = tile_masks(row_blocks, list_len, rows * nrows // TILE)
    own_mask = row_mask(tile_mask, lax.axis_index(ROW), rows)
    factor_mask = row_mask(tile_mask, lax.axis_index(ROW[:1] + COL[2:4]), rows)
    factor = jnp.stack([jnp.where(yh == 0, same, flip), jnp.where(yh == 0, flip, same)])
    factor = factor.reshape(2, sibs, width, rows) * factor_mask
    factor = jnp.broadcast_to(factor.reshape(2 * wide, rows), (nrows // 2, 2 * wide, rows))
    factor = exchange(factor, ROW[:2]).reshape(2, 2, nyl * wide, rows)

    ainv = ainv[None]
    for axis in ("xh", "xl", "core"):
        ainv = doubled(ainv, axis, 2 if axis == "core" else 0)
    panel_all = panel[None]
    for axis in ("ylh", "yll", "xh"):
        panel_all = doubled(panel_all, axis, 0)
    panel_far = lax.ppermute(panel_all, "xl", [(0, 1), (1, 0)])

    product = 0.0
    for high in range(2):
        for low in range(2):
            block = ainv[2 * low + high]
            product += lax.dot_general(
                factor[high, low], block, (((1,), (1,)), ((), ())), precision=HIGHEST
            )
    product = exchange(product.reshape(nyl, wide, rows), COL[2:4])
    plain = jnp.sum(product, axis=0)
    other = lax.ppermute(plain, "core", [(0, 1), (1, 0)])
    pair = [jnp.where(core == 0, plain, other), jnp.where(core == 0, other, plain)]
    pair = [block.reshape(sibs, width, rows) for block in pair]
    pair = -jnp.concatenate(pair, 1)
    half = lax.dynamic_slice_in_dim(pair, core * cols, cols, 2)
    pair = pair * own_mask

    terms = []
    for source in (panel_all, panel_far):
        source = source.reshape(2, 2, 2, sibs, width, rows)
        terms.append(jnp.einsum("ebdsvi,swi->edbsvw", source, pair, precision=HIGHEST))
    xl = lax.axis_index("xl")
    first = jnp.where(xl == 0, terms[0], terms[1])
    second = jnp.where(xl == 0, terms[1], terms[0])
    term = jnp.stack([first, second], 1)
    term = exchange(term.reshape(nrows, -1), ROW)
    own = lax.dynamic_slice_in_dim(kk_inverse, core * width, width, 1)
    own = lax.dynamic_slice_in_dim(own, lax.axis_index(COL[:4]) * NCORE * width, NCORE * width, 2)
    diag = own.reshape(-1) - jnp.sum(term, axis=0)

    ainv_ki = lax.ppermute(half, ROW + COL, transposed(nrows))
    tile = lax.dynamic_slice_in_dim(tile_mask, lax.axis_index(COL), 1, 1)
    ainv_ki = ainv_ki * tile[:, :, None]

    share = rows // ncols
    split = -plain.reshape(sibs, width, rows) * own_mask
    split = split.reshape(wide, ncols, share).transpose(1, 0, 2).reshape(ncols, -1, TILE)
    diag = diag.reshape(-1, TILE)
    mid = diag.shape[0]
    joined = jnp.concatenate([jnp.broadcast_to(diag, (ncols, *diag.shape)), split], 1)
    joined = jnp.pad(joined, ((0, 0), (0, -joined.shape[1] % 8), (0, 0)))
    joined = exchange(joined, COL)
    diag = joined[:, :mid].reshape(nchips, NCORE, sibs, width, NCORE * width)
    ainv_kk = diag.transpose(2, 1, 3, 0, 4).reshape(kk_inverse.shape)
    split = joined[:, mid : mid + wide * share // TILE].reshape(ncols, sibs, width, share)
    ainv_ik = split.transpose(3, 1, 0, 2).reshape(share, sibs, -1)
    return ainv_ik, ainv_kk, ainv_ki


def solution(mesh):
    devices = mesh.devices.reshape(4, 2, 2, 2, 2, 2, 2, 2)
    fine = Mesh(devices, ROW + COL)
    placed = (P(ROW, COL), P(ROW, None, COL), P(None, ROW, None), P(), P())

    return jax.shard_map(
        shards,
        mesh=fine,
        in_specs=placed,
        out_specs=(P(ROW + COL, None, None), P(None, ROW, None), P(None, ROW, COL)),
        check_vma=False,
    )
```

```python
import jax
import jax.numpy as jnp
from jax import lax
from jax.sharding import Mesh, PartitionSpec as P

TILE = 128
NCORE = 2
ROW = ("zh", "zl", "yh")
COL = ("xh", "xl", "ylh", "yll", "core")
HIGHEST = lax.Precision.HIGHEST


def tile_masks(row_blocks, list_len, ntiles):
    tiles = jnp.arange(ntiles, dtype=jnp.int32)
    valid = jnp.arange(row_blocks.shape[1], dtype=jnp.int32)[None, :] < list_len[:, None]
    hit = (row_blocks[:, :, None] == tiles[None, None, :]) & valid[:, :, None]
    return jnp.any(hit, axis=1).astype(jnp.float32)


def row_mask(tile_mask, row, rows):
    tiles = rows // TILE
    picked = lax.dynamic_slice_in_dim(tile_mask, row * tiles, tiles, 1)
    return jnp.repeat(picked, TILE, axis=1)[:, None, :]


def exchange(blocks, axes):
    return lax.all_to_all(blocks, axes, split_axis=0, concat_axis=0, tiled=True)


def doubled(block, axis, dim):
    other = lax.ppermute(block, axis, [(0, 1), (1, 0)])
    side = lax.axis_index(axis)
    first = jnp.where(side == 0, block, other)
    second = jnp.where(side == 0, other, block)
    return jnp.concatenate([first, second], dim)


def digit_swap(flip):
    zh, zl, yh = (lax.axis_size(a) for a in ROW)
    x, yl = lax.axis_size(COL[:2]), lax.axis_size(COL[2:4])
    pairs = []
    for a in range(zh):
        for b in range(zl * yh):
            for c in range(x):
                for d in range(yl):
                    for h in range(NCORE):
                        source = (((a * zl * yh + b) * x + c) * yl + d) * NCORE + h
                        target = (((a * yl + (d ^ flip)) * x + c) * zl * yh + b) * NCORE + h
                        pairs.append((source, target))
    return pairs


def transposed(nrows):
    return [
        ((r * nrows + q) * NCORE + h, (q * nrows + r) * NCORE + h)
        for r in range(nrows)
        for q in range(nrows)
        for h in range(NCORE)
    ]


def shards(ainv, lpanel, kk_inverse, row_blocks, list_len):
    nyl = lax.axis_size(COL[2:4])
    nrows, ncols = lax.axis_size(ROW), lax.axis_size(COL)
    nchips = ncols // NCORE
    rows, sibs, width = lpanel.shape
    cols = ainv.shape[1]
    wide = sibs * width
    core = lax.axis_index("core")

    panel = jnp.transpose(lpanel, (1, 2, 0)).reshape(wide, rows)
    yh = lax.axis_index("yh")
    same = lax.ppermute(panel, ROW + COL, digit_swap(0))
    flip = lax.ppermute(panel, ROW + COL, digit_swap(1))

    tile_mask = tile_masks(row_blocks, list_len, rows * nrows // TILE)
    own_mask = row_mask(tile_mask, lax.axis_index(ROW), rows)
    factor_mask = row_mask(tile_mask, lax.axis_index(ROW[:1] + COL[2:4]), rows)
    factor = jnp.stack([jnp.where(yh == 0, same, flip), jnp.where(yh == 0, flip, same)])
    factor = factor.reshape(2, sibs, width, rows) * factor_mask
    factor = jnp.broadcast_to(factor.reshape(2 * wide, rows), (nrows // 2, 2 * wide, rows))
    factor = exchange(factor, ROW[:2]).reshape(2, 2, nyl * wide, rows)

    ainv = ainv[None]
    for axis in ("xh", "xl", "core"):
        ainv = doubled(ainv, axis, 2 if axis == "core" else 0)
    panel_all = panel[None]
    for axis in ("ylh", "yll", "xh"):
        panel_all = doubled(panel_all, axis, 0)
    panel_far = lax.ppermute(panel_all, "xl", [(0, 1), (1, 0)])

    product = 0.0
    for high in range(2):
        for low in range(2):
            block = ainv[2 * low + high]
            product += lax.dot_general(
                factor[high, low], block, (((1,), (1,)), ((), ())), precision=HIGHEST
            )
    product = exchange(product.reshape(nyl, wide, rows), COL[2:4])
    plain = jnp.sum(product, axis=0).reshape(sibs, width, rows) * -own_mask
    other = lax.ppermute(plain, "core", [(0, 1), (1, 0)])
    pair = [jnp.where(core == 0, plain, other), jnp.where(core == 0, other, plain)]
    pair = jnp.concatenate(pair, 1)
    half = lax.dynamic_slice_in_dim(pair, core * cols, cols, 2)

    terms = []
    for source in (panel_all, panel_far):
        source = source.reshape(2, 2, 2, sibs, width, rows)
        terms.append(jnp.einsum("ebdsvi,swi->edbsvw", source, pair, precision=HIGHEST))
    xl = lax.axis_index("xl")
    first = jnp.where(xl == 0, terms[0], terms[1])
    second = jnp.where(xl == 0, terms[1], terms[0])
    term = jnp.stack([first, second], 1)
    term = exchange(term.reshape(nrows, -1), ROW)
    own = lax.dynamic_slice_in_dim(kk_inverse, core * width, width, 1)
    own = lax.dynamic_slice_in_dim(own, lax.axis_index(COL[:4]) * NCORE * width, NCORE * width, 2)
    diag = own.reshape(-1) - jnp.sum(term, axis=0)

    ainv_ki = lax.ppermute(half, ROW + COL, transposed(nrows))
    tile = lax.dynamic_slice_in_dim(tile_mask, lax.axis_index(COL), 1, 1)
    ainv_ki = ainv_ki * tile[:, :, None]

    share = rows // ncols
    split = plain.reshape(wide, ncols, share)
    split = split.transpose(1, 0, 2).reshape(ncols, -1, TILE)
    diag = diag.reshape(-1, TILE)
    mid = diag.shape[0]
    joined = jnp.concatenate([jnp.broadcast_to(diag, (ncols, *diag.shape)), split], 1)
    joined = jnp.pad(joined, ((0, 0), (0, -joined.shape[1] % 8), (0, 0)))
    joined = exchange(joined, COL)
    diag = joined[:, :mid].reshape(nchips, NCORE, sibs, width, NCORE * width)
    ainv_kk = diag.transpose(2, 1, 3, 0, 4).reshape(kk_inverse.shape)
    split = joined[:, mid : mid + wide * share // TILE].reshape(ncols, sibs, width, share)
    ainv_ik = split.transpose(3, 1, 0, 2).reshape(share, sibs, -1)
    return ainv_ik, ainv_kk, ainv_ki


def solution(mesh):
    devices = mesh.devices.reshape(4, 2, 2, 2, 2, 2, 2, 2)
    fine = Mesh(devices, ROW + COL)
    placed = (P(ROW, COL), P(ROW, None, COL), P(None, ROW, None), P(), P())

    return jax.shard_map(
        shards,
        mesh=fine,
        in_specs=placed,
        out_specs=(P(ROW + COL, None, None), P(None, ROW, None), P(None, ROW, COL)),
        check_vma=False,
    )
```

```python
import jax
import jax.numpy as jnp
from jax import lax
from jax.sharding import Mesh, PartitionSpec as P

TILE = 128
NCORE = 2
ROW = ("zh", "zl", "yh")
COL = ("xh", "xl", "ylh", "yll", "core")
HIGHEST = lax.Precision.HIGHEST


def tile_masks(row_blocks, list_len, ntiles):
    tiles = jnp.arange(ntiles, dtype=jnp.int32)
    valid = jnp.arange(row_blocks.shape[1], dtype=jnp.int32)[None, :] < list_len[:, None]
    hit = (row_blocks[:, :, None] == tiles[None, None, :]) & valid[:, :, None]
    return jnp.any(hit, axis=1).astype(jnp.float32)


def row_mask(tile_mask, row, rows):
    tiles = rows // TILE
    picked = lax.dynamic_slice_in_dim(tile_mask, row * tiles, tiles, 1)
    return jnp.repeat(picked, TILE, axis=1)[:, None, :]


def exchange(blocks, axes):
    return lax.all_to_all(blocks, axes, split_axis=0, concat_axis=0, tiled=True)


def doubled(block, axis, dim):
    other = lax.ppermute(block, axis, [(0, 1), (1, 0)])
    side = lax.axis_index(axis)
    first = jnp.where(side == 0, block, other)
    second = jnp.where(side == 0, other, block)
    return jnp.concatenate([first, second], dim)


def digit_swap(flip):
    zh, zl, yh = (lax.axis_size(a) for a in ROW)
    x, yl = lax.axis_size(COL[:2]), lax.axis_size(COL[2:4])
    pairs = []
    for a in range(zh):
        for b in range(zl * yh):
            for c in range(x):
                for d in range(yl):
                    for h in range(NCORE):
                        source = (((a * zl * yh + b) * x + c) * yl + d) * NCORE + h
                        target = (((a * yl + (d ^ flip)) * x + c) * zl * yh + b) * NCORE + h
                        pairs.append((source, target))
    return pairs


def transposed(nrows):
    return [
        ((r * nrows + q) * NCORE + h, (q * nrows + r) * NCORE + h)
        for r in range(nrows)
        for q in range(nrows)
        for h in range(NCORE)
    ]


def shards(ainv, lpanel, kk_inverse, row_blocks, list_len):
    nyl = lax.axis_size(COL[2:4])
    nrows, ncols = lax.axis_size(ROW), lax.axis_size(COL)
    nchips = ncols // NCORE
    rows, sibs, width = lpanel.shape
    cols = ainv.shape[1]
    wide = sibs * width
    core = lax.axis_index("core")

    panel = jnp.transpose(lpanel, (1, 2, 0)).reshape(wide, rows)
    yh = lax.axis_index("yh")
    same = lax.ppermute(panel, ROW + COL, digit_swap(0))
    flip = lax.ppermute(panel, ROW + COL, digit_swap(1))

    tile_mask = tile_masks(row_blocks, list_len, rows * nrows // TILE)
    own_mask = row_mask(tile_mask, lax.axis_index(ROW), rows)
    factor_mask = row_mask(tile_mask, lax.axis_index(ROW[:1] + COL[2:4]), rows)
    factor = jnp.stack([jnp.where(yh == 0, same, flip), jnp.where(yh == 0, flip, same)])
    factor = factor.reshape(2, sibs, width, rows) * factor_mask
    factor = jnp.broadcast_to(factor.reshape(2 * wide, rows), (nrows // 2, 2 * wide, rows))
    factor = exchange(factor, ROW[:2]).reshape(2, 2, nyl * wide, rows)

    ainv = ainv[None]
    for axis in ("xh", "xl", "core"):
        ainv = doubled(ainv, axis, 2 if axis == "core" else 0)
    panel_all = panel[None]
    for axis in ("ylh", "yll", "xh"):
        panel_all = doubled(panel_all, axis, 0)
    panel_far = lax.ppermute(panel_all, "xl", [(0, 1), (1, 0)])

    product = 0.0
    for high in range(2):
        for low in range(2):
            block = ainv[2 * low + high]
            product += lax.dot_general(
                factor[high, low], block, (((1,), (1,)), ((), ())), precision=HIGHEST
            )
    product = exchange(product.reshape(nyl, wide, rows), COL[2:4])
    plain = jnp.sum(product, axis=0).reshape(sibs, width, rows) * -own_mask
    other = lax.ppermute(plain, "core", [(0, 1), (1, 0)])
    pair = [jnp.where(core == 0, plain, other), jnp.where(core == 0, other, plain)]
    pair = jnp.concatenate(pair, 1)
    half = lax.dynamic_slice_in_dim(pair, core * cols, cols, 2)

    terms = []
    for source in (panel_all, panel_far):
        source = source.reshape(2, 2, 2, sibs, width, rows)
        terms.append(jnp.einsum("ebdsvi,swi->edbsvw", source, pair, precision=HIGHEST))
    xl = lax.axis_index("xl")
    first = jnp.where(xl == 0, terms[0], terms[1])
    second = jnp.where(xl == 0, terms[1], terms[0])
    term = jnp.stack([first, second], 1)
    term = term.reshape(nrows, -1, TILE)
    mid = term.shape[1]
    term = jnp.pad(term, ((0, 0), (0, -mid % 8), (0, 0)))
    term = exchange(term, ROW)
    own = lax.dynamic_slice_in_dim(kk_inverse, core * width, width, 1)
    own = lax.dynamic_slice_in_dim(own, lax.axis_index(COL[:4]) * NCORE * width, NCORE * width, 2)
    diag = own.reshape(mid, TILE) - jnp.sum(term, axis=0)[:mid]

    ainv_ki = lax.ppermute(half, ROW + COL, transposed(nrows))
    tile = lax.dynamic_slice_in_dim(tile_mask, lax.axis_index(COL), 1, 1)
    ainv_ki = ainv_ki * tile[:, :, None]

    share = rows // ncols
    split = plain.reshape(wide, ncols, share)
    split = split.transpose(1, 0, 2).reshape(ncols, -1, TILE)
    joined = jnp.concatenate([jnp.broadcast_to(diag, (ncols, *diag.shape)), split], 1)
    joined = jnp.pad(joined, ((0, 0), (0, -joined.shape[1] % 8), (0, 0)))
    joined = exchange(joined, COL)
    diag = joined[:, :mid].reshape(nchips, NCORE, sibs, width, NCORE * width)
    ainv_kk = diag.transpose(2, 1, 3, 0, 4).reshape(kk_inverse.shape)
    split = joined[:, mid : mid + wide * share // TILE].reshape(ncols, sibs, width, share)
    ainv_ik = split.transpose(3, 1, 0, 2).reshape(share, sibs, -1)
    return ainv_ik, ainv_kk, ainv_ki


def solution(mesh):
    devices = mesh.devices.reshape(4, 2, 2, 2, 2, 2, 2, 2)
    fine = Mesh(devices, ROW + COL)
    placed = (P(ROW, COL), P(ROW, None, COL), P(None, ROW, None), P(), P())

    return jax.shard_map(
        shards,
        mesh=fine,
        in_specs=placed,
        out_specs=(P(ROW + COL, None, None), P(None, ROW, None), P(None, ROW, COL)),
        check_vma=False,
    )
```
